256 devices in a mesh: leaf: 4 (over x), owner: 64 (over z, y, core).
Axes of the slice: x: 4, y: 4, z: 8, core: 2. Of those that a mesh axis runs over, the one named last changes fastest.
Arguments:
- multipoles: float32 [3, 343, 98304], P(None, None, ('leaf', 'owner')), may hold values from -6 to 6
- operators: bfloat16 [4, 1029, 1029], replicated, may hold values from -0.1875 to 0.1875
- lists: int32 [98304, 4], P(('leaf', 'owner')), may hold values from -1 to 671, as said below
- send_slots: int32 [256, 64, 4], P(('leaf', 'owner')), may hold values from -1 to 31, as said below
Outputs:
- locals_out: float32 [3, 343, 98304], P(None, None, ('leaf', 'owner'))
The draws below stay inside these ranges and needn't reach their ends.
Inputs may be any that keep to these rules, and one draw needn't show every extreme that they name: `lists`: A code of the first kind appears only for boxes of groups other than the first, of the third kind only for groups other than the last; a code naming (p, c) appears only where send_slots of owner p for this owner holds a slot at c, and never with p equal to the box's own owner. `send_slots`: entries are distinct boundary slots followed by -1 padding; the entries for an owner itself are all -1; every draw fills some pair's 4 entries.
All inputs are finite; a program needn't handle non-finite values.
Results may differ from the reference program's by a relative error of at most 0.0029.
Values may be sent and summed in bfloat16 or wider, within the bound.
No kernel may reach another device: no remote copies, remote signals or barrier semaphores. Data moves between devices by JAX's collectives and lax.ppermute only.
A program may use at most 128 MiB of HBM per device.

```python
import jax
import jax.numpy as jnp

COMP = 3
NODES = 343
DIRS = 4
BOX_DEV = 384
FACE = 16
BOUND = 32
CAP = 4
GROUPS = 4
OWNERS = 64
DEVS = 256
BOXES = 98304


def joint_tables(key):
    base = jax.random.fold_in(key, 31)
    keys = jax.random.split(base, 11)
    scores = jax.random.randint(keys[0], (DEVS, OWNERS, BOUND), 0, BOUND) * BOUND + jnp.arange(BOUND, dtype=jnp.int32)
    order = jnp.argsort(scores, axis=-1)[:, :, :CAP].astype(jnp.int32)
    sender = jnp.arange(DEVS, dtype=jnp.int32)[:, None]
    peer = jnp.arange(OWNERS, dtype=jnp.int32)[None, :]
    receiver = sender // OWNERS * OWNERS + peer
    hotness = jax.random.randint(keys[1], (DEVS,), 0, CAP + 1)
    drawn = jax.random.randint(keys[2], (DEVS, OWNERS), 0, CAP + 1)
    count = jnp.minimum(CAP, drawn + hotness[receiver])
    chosen_sender = jax.random.randint(keys[3], (), 0, DEVS)
    chosen_peer = (chosen_sender % OWNERS + 1 + jax.random.randint(keys[4], (), 0, OWNERS - 1)) % OWNERS
    forced = (sender == chosen_sender) & (peer == chosen_peer)
    count = jnp.where(forced, CAP, count)
    count = jnp.where(peer == sender % OWNERS, 0, count)
    places = jnp.arange(CAP, dtype=jnp.int32)[None, None, :]
    provided = jnp.where(places < count[:, :, None], order, -1).astype(jnp.int32)
    shape = (DEVS, BOX_DEV, DIRS)
    device = jnp.arange(DEVS, dtype=jnp.int32)[:, None, None]
    group = device // OWNERS
    mine = jnp.broadcast_to(device % OWNERS, shape)
    kind = jax.random.randint(keys[5], shape, 0, 20)
    local_code = FACE + jax.random.randint(keys[6], shape, 0, BOX_DEV)
    side_low = jax.random.randint(keys[7], shape, 0, 2) == 0
    rim = jax.random.randint(keys[8], shape, 0, FACE)
    halo_code = jnp.where(side_low, rim, FACE + BOX_DEV + rim)
    halo_ok = jnp.where(side_low, group > 0, group < GROUPS - 1)
    other = jax.random.randint(keys[9], shape, 0, OWNERS)
    column = jax.random.randint(keys[10], shape, 0, CAP)
    source_dev = group * OWNERS + other
    slot = provided[source_dev, mine, column]
    ghost_code = 2 * FACE + BOX_DEV + other * CAP + column
    code = local_code
    code = jnp.where((kind >= 10) & (kind < 13) & halo_ok, halo_code, code)
    code = jnp.where((kind >= 13) & (slot >= 0), ghost_code, code)
    code = jnp.where(kind < 3, -1, code)
    return (provided, code.reshape(DEVS * BOX_DEV, DIRS).astype(jnp.int32))


def draw_lists(key, part):
    return joint_tables(key)[1]


def draw_send_slots(key, part):
    return joint_tables(key)[0]


def block_levels(stream_key, shape, cuts, low, largest):
    factor_of = 1.0
    for dim, blocks in cuts:
        steps = jax.random.uniform(jax.random.fold_in(jax.random.fold_in(stream_key, 6), dim), (blocks,), jnp.float32, low / len(cuts), largest / len(cuts))
        factor_of = factor_of * jnp.repeat(jnp.exp(steps), shape[dim] // blocks).reshape((-1,) + (1,) * (len(shape) - 1 - dim))
    return factor_of


def bell_draw(key, extent, scale, most, pieces=(), held_as=jnp.bfloat16):
    drawn = scale * jax.random.normal(key, extent, jnp.float32)
    if pieces:
        drawn = drawn * block_levels(key, extent, pieces, -0.22, 0.18)
    return jnp.clip(drawn, -most, most).astype(held_as)


def setup_inputs(seed: int = 0) -> dict:
    streams_of = jax.random.split(jax.random.key(seed), 5)
    multipoles = bell_draw(streams_of[0], (COMP, NODES, BOXES), 1.0, 6.0, ((2, 256),), jnp.float32)
    operators = bell_draw(streams_of[1], (DIRS, COMP * NODES, COMP * NODES), (COMP * NODES) ** -0.5, 0.1875)
    lists = draw_lists(jax.random.fold_in(streams_of[4], 71), 0)
    send_slots = draw_send_slots(jax.random.fold_in(streams_of[4], 71), 0)
    return {"multipoles": multipoles, "operators": operators, "lists": lists, "send_slots": send_slots}


def reference(multipoles, operators, lists, send_slots):
    width = COMP * NODES
    packed = multipoles.reshape(width, BOXES).astype(jnp.bfloat16)
    rows = jnp.arange(BOXES, dtype=jnp.int32)[:, None]
    device = rows // BOX_DEV
    group = device // OWNERS
    mine = device % OWNERS
    code = lists
    lower = (device - OWNERS) * BOX_DEV + BOX_DEV - FACE + code
    here = device * BOX_DEV + code - FACE
    upper = (device + OWNERS) * BOX_DEV + code - FACE - BOX_DEV
    ghost = jnp.maximum(code - 2 * FACE - BOX_DEV, 0)
    peer = ghost // CAP
    column = ghost % CAP
    provider = group * OWNERS + peer
    slot = send_slots[jnp.clip(provider, 0, DEVS - 1), jnp.broadcast_to(mine, code.shape), column]
    remote = provider * BOX_DEV + jnp.maximum(slot, 0)
    target = jnp.where(code < FACE, lower, jnp.where(code < FACE + BOX_DEV, here, jnp.where(code < 2 * FACE + BOX_DEV, upper, remote)))
    valid = code >= 0
    valid = valid & jnp.where(code < FACE, group > 0, True)
    valid = valid & jnp.where((code >= FACE + BOX_DEV) & (code < 2 * FACE + BOX_DEV), group < GROUPS - 1, True)
    target = jnp.where(valid, target, 0).astype(jnp.int32)
    total = jnp.zeros((width, BOXES), jnp.float32)
    for direction in range(DIRS):
        present = valid[:, direction].astype(jnp.bfloat16)
        columns = jnp.take(packed, target[:, direction], axis=1) * present[None, :]
        total = total + jnp.dot(operators[direction], columns, preferred_element_type=jnp.float32)
    return total.reshape(COMP, NODES, BOXES)
```

```python
import jax
import jax.numpy as jnp
from jax import lax
from jax.experimental import pallas as pl
from jax.experimental.pallas import tpu as pltpu
from jax.sharding import PartitionSpec as P

FACE = 16
LANES = 128
NT = (((1,), (1,)), ((), ()))


def table_kernel(first_ref, last_ref, slots_ref, table_ref, low_ref, high_ref, stage):
    comps, nodes, lanes = first_ref.shape
    cap, owners = slots_ref.shape
    rows = owners * cap
    for comp in range(comps):
        stage[pl.ds(comp * nodes, nodes), :lanes] = first_ref[comp]
        stage[pl.ds(comp * nodes, nodes), lanes:] = last_ref[comp]
    boundary = stage[...].astype(jnp.bfloat16)
    row = lax.broadcasted_iota(jnp.int32, (rows, owners), 0)
    owner = lax.broadcasted_iota(jnp.int32, (rows, owners), 1)
    spread = (row // cap == owner).astype(jnp.bfloat16)
    slots = slots_ref[...].astype(jnp.float32).astype(jnp.bfloat16)
    every = lax.dot_general(spread, slots, NT, preferred_element_type=jnp.float32)
    place = lax.broadcasted_iota(jnp.int32, (rows, cap), 1)
    turn = lax.broadcasted_iota(jnp.int32, (rows, cap), 0) % cap
    wanted = jnp.sum(jnp.where(place == turn, every, 0.0), axis=1, keepdims=True)
    slot = lax.broadcasted_iota(jnp.int32, (rows, 2 * lanes), 1).astype(jnp.float32)
    pick = (slot == wanted).astype(jnp.bfloat16)
    column = lax.broadcasted_iota(jnp.int32, (2 * FACE, 2 * lanes), 1)
    face = lax.broadcasted_iota(jnp.int32, (2 * FACE, 2 * lanes), 0)
    face = jnp.where(face < FACE, face + (2 * lanes - FACE), face - FACE)
    pick = jnp.concatenate([pick, (column == face).astype(jnp.bfloat16)], axis=0)
    table = lax.dot_general(pick, boundary, NT, preferred_element_type=jnp.float32).astype(jnp.bfloat16)
    table_ref[...] = table[:rows].reshape(table_ref.shape)
    low_ref[...] = table[rows:rows + FACE]
    high_ref[...] = table[rows + FACE:]


def make_table(multipoles, slots):
    comps, nodes, nboxes = multipoles.shape
    cap, owners = slots.shape
    width = comps * nodes
    last = nboxes // LANES - 1
    return pl.pallas_call(
        table_kernel,
        out_shape=(
            jax.ShapeDtypeStruct((owners, cap, width), jnp.bfloat16),
            jax.ShapeDtypeStruct((FACE, width), jnp.bfloat16),
            jax.ShapeDtypeStruct((FACE, width), jnp.bfloat16),
        ),
        grid=(1,),
        in_specs=[
            pl.BlockSpec((comps, nodes, LANES), lambda i: (0, 0, 0)),
            pl.BlockSpec((comps, nodes, LANES), lambda i: (0, 0, last)),
            pl.BlockSpec((cap, owners), lambda i: (0, 0)),
        ],
        out_specs=(
            pl.BlockSpec((owners, cap, width), lambda i: (0, 0, 0)),
            pl.BlockSpec((FACE, width), lambda i: (0, 0)),
            pl.BlockSpec((FACE, width), lambda i: (0, 0)),
        ),
        scratch_shapes=[pltpu.VMEM((width, 2 * LANES), jnp.float32)],
        name="table",
    )(multipoles, multipoles, slots)


def spread_out(y, spread, comp):
    for t in range(spread.shape[1]):
        spread[comp, t] = y[:, t * LANES:(t + 1) * LANES]


def gather_in(spread, picks, comp, dirs, nodes):
    pieces = [
        spread[comp, t, pl.ds(d, nodes, stride=dirs), :]
        for d in range(dirs)
        for t in range(spread.shape[1])
    ]
    moved = jnp.concatenate(pieces, axis=1).astype(jnp.bfloat16)
    return jnp.dot(moved, picks[...], preferred_element_type=jnp.float32)


def near_kernel(m_hbm, low_ref, high_ref, codes_ref, a_hbm, near_hbm, stage, source, picks, spread, held, total, sems, m_sems, out_sems):
    comps, nodes, nboxes = m_hbm.shape
    dirs, width = a_hbm.shape[1:]
    wide = picks.shape[0] // dirs

    def fetch(comp):
        return pltpu.make_async_copy(a_hbm.at[pl.ds(comp * nodes, nodes)], held.at[comp], sems.at[comp])

    def fetch_m(comp):
        return pltpu.make_async_copy(m_hbm.at[comp], total.at[comp], m_sems.at[comp])

    def store(comp):
        return pltpu.make_async_copy(total.at[comp], near_hbm.at[comp], out_sems.at[comp])

    for comp in range(comps):
        fetch_m(comp).start()
    for comp in range(comps):
        fetch(comp).start()
    blank = jnp.zeros((wide - nboxes - 2 * FACE, width), jnp.bfloat16)
    source[:, nboxes:] = jnp.concatenate([low_ref[...], high_ref[...], blank], axis=0).T
    place = lax.broadcasted_iota(jnp.int32, (wide, nboxes), 0)
    for d in range(dirs):
        code = codes_ref[pl.ds(d, 1), :]
        low = jnp.where(code < FACE, code + nboxes, code - FACE)
        wanted = jnp.where(code < nboxes + FACE, low, code)
        wanted = jnp.where((code < 0) | (code >= nboxes + 2 * FACE), -1, wanted)
        picks[pl.ds(d * wide, wide), :] = (place == wanted).astype(jnp.bfloat16)
    for comp in range(comps):
        fetch_m(comp).wait()
        stage[pl.ds(comp * nodes, nodes), :] = total[comp]
    source[:, :nboxes] = stage[...].astype(jnp.bfloat16)

    @pl.loop(0, comps)
    def _(comp):
        fetch(comp).wait()
        a = held[comp].reshape(nodes * dirs, width)
        spread_out(jnp.dot(a, source[...], preferred_element_type=jnp.float32), spread, comp)

    @pl.loop(0, comps)
    def _(comp):
        total[comp] = gather_in(spread, picks, comp, dirs, nodes)
        store(comp).start()

    @pl.loop(0, comps)
    def _(comp):
        store(comp).wait()


def far_kernel(near_hbm, g_ref, codes_ref, a_hbm, out_hbm, source, picks, spread, held, total, sems, near_sems, out_sems):
    comps, nodes, nboxes = near_hbm.shape
    dirs = a_hbm.shape[1]
    width = a_hbm.shape[2]
    wide = picks.shape[0] // dirs

    def fetch(comp):
        return pltpu.make_async_copy(a_hbm.at[pl.ds(comp * nodes, nodes)], held.at[comp], sems.at[comp])

    def fetch_near(comp):
        return pltpu.make_async_copy(near_hbm.at[comp], total.at[comp], near_sems.at[comp])

    def store(comp):
        return pltpu.make_async_copy(total.at[comp], out_hbm.at[comp], out_sems.at[comp])

    for comp in range(comps):
        fetch(comp).start()
    for comp in range(comps):
        fetch_near(comp).start()
    source[...] = g_ref[...].reshape(source.shape[1], source.shape[0]).T
    place = lax.broadcasted_iota(jnp.int32, (wide, nboxes), 0) + (nboxes + 2 * FACE)
    for d in range(dirs):
        picks[pl.ds(d * wide, wide), :] = (place == codes_ref[pl.ds(d, 1), :]).astype(jnp.bfloat16)

    @pl.loop(0, comps + 1)
    def _(comp):
        @pl.when(comp < comps)
        def _():
            fetch(comp).wait()
            a = held[comp].reshape(nodes * dirs, width)
            spread_out(jnp.dot(a, source[...], preferred_element_type=jnp.float32), spread, comp)

        @pl.when(comp > 0)
        def _():
            last = comp - 1
            fetch_near(last).wait()
            total[last] = total[last] + gather_in(spread, picks, last, dirs, nodes)
            store(last).start()

    @pl.loop(0, comps)
    def _(comp):
        store(comp).wait()


HBM = pl.BlockSpec(memory_space=pltpu.MemorySpace.HBM)
VMEM = pl.BlockSpec(memory_space=pltpu.MemorySpace.VMEM)


def near_sum(multipoles, low, high, codes, rows):
    comps, nodes, nboxes = multipoles.shape
    width, dirs, _ = rows.shape
    wide = nboxes + LANES
    return pl.pallas_call(
        near_kernel,
        out_shape=jax.ShapeDtypeStruct((comps, nodes, nboxes), jnp.float32),
        in_specs=[HBM, VMEM, VMEM, VMEM, HBM],
        out_specs=HBM,
        scratch_shapes=[
            pltpu.VMEM((width, nboxes), jnp.float32),
            pltpu.VMEM((width, wide), jnp.bfloat16),
            pltpu.VMEM((dirs * wide, nboxes), jnp.bfloat16),
            pltpu.VMEM((comps, wide // LANES, nodes * dirs, LANES), jnp.float32),
            pltpu.VMEM((comps, nodes, dirs, width), jnp.bfloat16),
            pltpu.VMEM((comps, nodes, nboxes), jnp.float32),
            pltpu.SemaphoreType.DMA((comps,)),
            pltpu.SemaphoreType.DMA((comps,)),
            pltpu.SemaphoreType.DMA((comps,)),
        ],
        compiler_params=pltpu.CompilerParams(vmem_limit_bytes=52 << 20),
        name="near",
    )(multipoles, low, high, codes, rows)


def far_sum(near, ghost, codes, rows):
    comps, nodes, nboxes = near.shape
    width, dirs, _ = rows.shape
    owners, cap, _ = ghost.shape
    wide = owners * cap
    return pl.pallas_call(
        far_kernel,
        out_shape=jax.ShapeDtypeStruct((comps, nodes, nboxes), jnp.float32),
        in_specs=[HBM, VMEM, VMEM, HBM],
        out_specs=HBM,
        scratch_shapes=[
            pltpu.VMEM((width, wide), jnp.bfloat16),
            pltpu.VMEM((dirs * wide, nboxes), jnp.bfloat16),
            pltpu.VMEM((comps, wide // LANES, nodes * dirs, LANES), jnp.float32),
            pltpu.VMEM((comps, nodes, dirs, width), jnp.bfloat16),
            pltpu.VMEM((comps, nodes, nboxes), jnp.float32),
            pltpu.SemaphoreType.DMA((comps,)),
            pltpu.SemaphoreType.DMA((comps,)),
            pltpu.SemaphoreType.DMA((comps,)),
        ],
        compiler_params=pltpu.CompilerParams(vmem_limit_bytes=52 << 20),
        name="far",
    )(near, ghost, codes, rows)


def local(multipoles, operators, lists, send_slots):
    slots = jnp.transpose(send_slots[0])
    table, low, high = make_table(multipoles, slots)
    ghost = lax.all_to_all(table, "owner", 0, 0, tiled=True)
    count = lax.axis_size("leaf")
    forward = [(i, i + 1) for i in range(count - 1)]
    backward = [(target, source) for source, target in forward]
    low = lax.ppermute(low, "leaf", forward)
    high = lax.ppermute(high, "leaf", backward)
    codes = jnp.transpose(lists)
    rows = jnp.transpose(operators, (1, 0, 2))
    near = near_sum(multipoles, low, high, codes, rows)
    return far_sum(near, ghost, codes, rows)


def solution(mesh):
    return jax.shard_map(
        local,
        mesh=mesh,
        in_specs=(
            P(None, None, ("leaf", "owner")),
            P(),
            P(("leaf", "owner"), None),
            P(("leaf", "owner"), None, None),
        ),
        out_specs=P(None, None, ("leaf", "owner")),
        check_vma=False,
    )
```

```python
import jax
import jax.numpy as jnp
from jax import lax
from jax.experimental import pallas as pl
from jax.experimental.pallas import tpu as pltpu
from jax.sharding import PartitionSpec as P

FACE = 16
LANES = 128
NT = (((1,), (1,)), ((), ()))


def table_kernel(first_ref, last_ref, slots_ref, table_ref, low_ref, high_ref, stage):
    comps, nodes, lanes = first_ref.shape
    cap, owners = slots_ref.shape
    rows = owners * cap
    for comp in range(comps):
        stage[pl.ds(comp * nodes, nodes), :lanes] = first_ref[comp]
        stage[pl.ds(comp * nodes, nodes), lanes:] = last_ref[comp]
    boundary = stage[...].astype(jnp.bfloat16)
    row = lax.broadcasted_iota(jnp.int32, (rows, owners), 0)
    owner = lax.broadcasted_iota(jnp.int32, (rows, owners), 1)
    spread = (row // cap == owner).astype(jnp.bfloat16)
    slots = slots_ref[...].astype(jnp.float32).astype(jnp.bfloat16)
    every = lax.dot_general(spread, slots, NT, preferred_element_type=jnp.float32)
    place = lax.broadcasted_iota(jnp.int32, (rows, cap), 1)
    turn = lax.broadcasted_iota(jnp.int32, (rows, cap), 0) % cap
    wanted = jnp.sum(jnp.where(place == turn, every, 0.0), axis=1, keepdims=True)
    slot = lax.broadcasted_iota(jnp.int32, (rows, 2 * lanes), 1).astype(jnp.float32)
    pick = (slot == wanted).astype(jnp.bfloat16)
    column = lax.broadcasted_iota(jnp.int32, (2 * FACE, 2 * lanes), 1)
    face = lax.broadcasted_iota(jnp.int32, (2 * FACE, 2 * lanes), 0)
    face = jnp.where(face < FACE, face + (2 * lanes - FACE), face - FACE)
    pick = jnp.concatenate([pick, (column == face).astype(jnp.bfloat16)], axis=0)
    table = lax.dot_general(pick, boundary, NT, preferred_element_type=jnp.float32).astype(jnp.bfloat16)
    table_ref[...] = table[:rows].reshape(table_ref.shape)
    low_ref[...] = table[rows:rows + FACE]
    high_ref[...] = table[rows + FACE:]


def make_table(multipoles, slots):
    comps, nodes, nboxes = multipoles.shape
    cap, owners = slots.shape
    width = comps * nodes
    last = nboxes // LANES - 1
    return pl.pallas_call(
        table_kernel,
        out_shape=(
            jax.ShapeDtypeStruct((owners, cap, width), jnp.bfloat16),
            jax.ShapeDtypeStruct((FACE, width), jnp.bfloat16),
            jax.ShapeDtypeStruct((FACE, width), jnp.bfloat16),
        ),
        grid=(1,),
        in_specs=[
            pl.BlockSpec((comps, nodes, LANES), lambda i: (0, 0, 0)),
            pl.BlockSpec((comps, nodes, LANES), lambda i: (0, 0, last)),
            pl.BlockSpec((cap, owners), lambda i: (0, 0)),
        ],
        out_specs=(
            pl.BlockSpec((owners, cap, width), lambda i: (0, 0, 0)),
            pl.BlockSpec((FACE, width), lambda i: (0, 0)),
            pl.BlockSpec((FACE, width), lambda i: (0, 0)),
        ),
        scratch_shapes=[pltpu.VMEM((width, 2 * LANES), jnp.float32)],
        name="table",
    )(multipoles, multipoles, slots)


def spread_out(y, spread, comp):
    for t in range(spread.shape[1]):
        spread[comp, t] = y[:, t * LANES:(t + 1) * LANES]


def gather_in(total, spread, picks, comp, dirs, nodes):
    tiles = spread.shape[1]
    wide = tiles * LANES
    for d in range(dirs):
        pieces = [spread[comp, t, pl.ds(d, nodes, stride=dirs), :] for t in range(tiles)]
        moved = jnp.concatenate(pieces, axis=1).astype(jnp.bfloat16)
        part = jnp.dot(moved, picks[pl.ds(d * wide, wide), :], preferred_element_type=jnp.float32)
        total = part if total is None else total + part
    return total


def near_kernel(m_ref, low_ref, high_ref, codes_ref, a_hbm, near_hbm, stage, source, picks, spread, held, total, sems, out_sems):
    comps, nodes, nboxes = m_ref.shape
    dirs, width = a_hbm.shape[1:]
    wide = picks.shape[0] // dirs

    def fetch(comp):
        return pltpu.make_async_copy(a_hbm.at[pl.ds(comp * nodes, nodes)], held.at[comp], sems.at[comp])

    def store(comp):
        return pltpu.make_async_copy(total.at[comp], near_hbm.at[comp], out_sems.at[comp])

    for comp in range(comps):
        fetch(comp).start()
    blank = jnp.zeros((wide - nboxes - 2 * FACE, width), jnp.bfloat16)
    source[:, nboxes:] = jnp.concatenate([low_ref[...], high_ref[...], blank], axis=0).T
    place = lax.broadcasted_iota(jnp.int32, (wide, nboxes), 0)
    for d in range(dirs):
        code = codes_ref[pl.ds(d, 1), :]
        low = jnp.where(code < FACE, code + nboxes, code - FACE)
        wanted = jnp.where(code < nboxes + FACE, low, code)
        wanted = jnp.where((code < 0) | (code >= nboxes + 2 * FACE), -1, wanted)
        picks[pl.ds(d * wide, wide), :] = (place == wanted).astype(jnp.bfloat16)
    for comp in range(comps):
        stage[pl.ds(comp * nodes, nodes), :] = m_ref[comp]
    source[:, :nboxes] = stage[...].astype(jnp.bfloat16)

    @pl.loop(0, comps)
    def _(comp):
        fetch(comp).wait()
        a = held[comp].reshape(nodes * dirs, width)
        spread_out(jnp.dot(a, source[...], preferred_element_type=jnp.float32), spread, comp)

    for comp in range(comps):
        total[comp] = gather_in(None, spread, picks, comp, dirs, nodes)
        store(comp).start()
    for comp in range(comps):
        store(comp).wait()


def far_kernel(near_hbm, g_ref, codes_ref, a_hbm, out_hbm, source, picks, spread, held, total, sems, near_sems, out_sems):
    comps, nodes, nboxes = near_hbm.shape
    dirs = a_hbm.shape[1]
    width = a_hbm.shape[2]
    wide = picks.shape[0] // dirs

    def fetch(comp):
        return pltpu.make_async_copy(a_hbm.at[pl.ds(comp * nodes, nodes)], held.at[comp], sems.at[comp])

    def fetch_near(comp):
        return pltpu.make_async_copy(near_hbm.at[comp], total.at[comp], near_sems.at[comp])

    def store(comp):
        return pltpu.make_async_copy(total.at[comp], out_hbm.at[comp], out_sems.at[comp])

    for comp in range(comps):
        fetch(comp).start()
    for comp in range(comps):
        fetch_near(comp).start()
    source[...] = g_ref[...].reshape(source.shape[1], source.shape[0]).T
    place = lax.broadcasted_iota(jnp.int32, (wide, nboxes), 0) + (nboxes + 2 * FACE)
    for d in range(dirs):
        picks[pl.ds(d * wide, wide), :] = (place == codes_ref[pl.ds(d, 1), :]).astype(jnp.bfloat16)

    @pl.loop(0, comps)
    def _(comp):
        fetch(comp).wait()
        a = held[comp].reshape(nodes * dirs, width)
        spread_out(jnp.dot(a, source[...], preferred_element_type=jnp.float32), spread, comp)

    for comp in range(comps):
        fetch_near(comp).wait()
        total[comp] = gather_in(total[comp], spread, picks, comp, dirs, nodes)
        store(comp).start()
    for comp in range(comps):
        store(comp).wait()


HBM = pl.BlockSpec(memory_space=pltpu.MemorySpace.HBM)
VMEM = pl.BlockSpec(memory_space=pltpu.MemorySpace.VMEM)


def near_sum(multipoles, low, high, codes, rows):
    comps, nodes, nboxes = multipoles.shape
    width, dirs, _ = rows.shape
    wide = nboxes + LANES
    return pl.pallas_call(
        near_kernel,
        out_shape=pltpu.MemorySpace.HBM((comps, nodes, nboxes), jnp.float32),
        in_specs=[VMEM, VMEM, VMEM, VMEM, HBM],
        out_specs=HBM,
        scratch_shapes=[
            pltpu.VMEM((width, nboxes), jnp.float32),
            pltpu.VMEM((width, wide), jnp.bfloat16),
            pltpu.VMEM((dirs * wide, nboxes), jnp.bfloat16),
            pltpu.VMEM((comps, wide // LANES, nodes * dirs, LANES), jnp.float32),
            pltpu.VMEM((comps, nodes, dirs, width), jnp.bfloat16),
            pltpu.VMEM((comps, nodes, nboxes), jnp.float32),
            pltpu.SemaphoreType.DMA((comps,)),
            pltpu.SemaphoreType.DMA((comps,)),
        ],
        compiler_params=pltpu.CompilerParams(vmem_limit_bytes=52 << 20),
        name="near",
    )(multipoles, low, high, codes, rows)


def far_sum(near, ghost, codes, rows):
    comps, nodes, nboxes = near.shape
    width, dirs, _ = rows.shape
    owners, cap, _ = ghost.shape
    wide = owners * cap
    return pl.pallas_call(
        far_kernel,
        out_shape=jax.ShapeDtypeStruct((comps, nodes, nboxes), jnp.float32),
        in_specs=[HBM, VMEM, VMEM, HBM],
        out_specs=HBM,
        scratch_shapes=[
            pltpu.VMEM((width, wide), jnp.bfloat16),
            pltpu.VMEM((dirs * wide, nboxes), jnp.bfloat16),
            pltpu.VMEM((comps, wide // LANES, nodes * dirs, LANES), jnp.float32),
            pltpu.VMEM((comps, nodes, dirs, width), jnp.bfloat16),
            pltpu.VMEM((comps, nodes, nboxes), jnp.float32),
            pltpu.SemaphoreType.DMA((comps,)),
            pltpu.SemaphoreType.DMA((comps,)),
            pltpu.SemaphoreType.DMA((comps,)),
        ],
        compiler_params=pltpu.CompilerParams(vmem_limit_bytes=52 << 20),
        name="far",
    )(near, ghost, codes, rows)


def local(multipoles, operators, lists, send_slots):
    slots = jnp.transpose(send_slots[0])
    table, low, high = make_table(multipoles, slots)
    ghost = lax.all_to_all(table, "owner", 0, 0, tiled=True)
    count = lax.axis_size("leaf")
    forward = [(i, i + 1) for i in range(count - 1)]
    backward = [(target, source) for source, target in forward]
    low = lax.ppermute(low, "leaf", forward)
    high = lax.ppermute(high, "leaf", backward)
    codes = jnp.transpose(lists)
    rows = jnp.transpose(operators, (1, 0, 2))
    near = near_sum(multipoles, low, high, codes, rows)
    return far_sum(near, ghost, codes, rows)


def solution(mesh):
    return jax.shard_map(
        local,
        mesh=mesh,
        in_specs=(
            P(None, None, ("leaf", "owner")),
            P(),
            P(("leaf", "owner"), None),
            P(("leaf", "owner"), None, None),
        ),
        out_specs=P(None, None, ("leaf", "owner")),
        check_vma=False,
    )
```

```python
import jax
import jax.numpy as jnp
from jax import lax
from jax.experimental import pallas as pl
from jax.experimental.pallas import tpu as pltpu
from jax.sharding import PartitionSpec as P

FACE = 16
LANES = 128
NT = (((1,), (1,)), ((), ()))


def table_kernel(first_ref, last_ref, slots_ref, table_ref, low_ref, high_ref, stage):
    comps, nodes, lanes = first_ref.shape
    cap, owners = slots_ref.shape
    rows = owners * cap
    for comp in range(comps):
        stage[pl.ds(comp * nodes, nodes), :lanes] = first_ref[comp]
        stage[pl.ds(comp * nodes, nodes), lanes:] = last_ref[comp]
    boundary = stage[...].astype(jnp.bfloat16)
    row = lax.broadcasted_iota(jnp.int32, (rows, owners), 0)
    owner = lax.broadcasted_iota(jnp.int32, (rows, owners), 1)
    spread = (row // cap == owner).astype(jnp.bfloat16)
    slots = slots_ref[...].astype(jnp.float32).astype(jnp.bfloat16)
    every = lax.dot_general(spread, slots, NT, preferred_element_type=jnp.float32)
    place = lax.broadcasted_iota(jnp.int32, (rows, cap), 1)
    turn = lax.broadcasted_iota(jnp.int32, (rows, cap), 0) % cap
    wanted = jnp.sum(jnp.where(place == turn, every, 0.0), axis=1, keepdims=True)
    slot = lax.broadcasted_iota(jnp.int32, (rows, 2 * lanes), 1).astype(jnp.float32)
    pick = (slot == wanted).astype(jnp.bfloat16)
    column = lax.broadcasted_iota(jnp.int32, (2 * FACE, 2 * lanes), 1)
    face = lax.broadcasted_iota(jnp.int32, (2 * FACE, 2 * lanes), 0)
    face = jnp.where(face < FACE, face + (2 * lanes - FACE), face - FACE)
    pick = jnp.concatenate([pick, (column == face).astype(jnp.bfloat16)], axis=0)
    table = lax.dot_general(pick, boundary, NT, preferred_element_type=jnp.float32).astype(jnp.bfloat16)
    table_ref[...] = table[:rows].reshape(table_ref.shape)
    low_ref[...] = table[rows:rows + FACE]
    high_ref[...] = table[rows + FACE:]


def make_table(multipoles, slots):
    comps, nodes, nboxes = multipoles.shape
    cap, owners = slots.shape
    width = comps * nodes
    last = nboxes // LANES - 1
    return pl.pallas_call(
        table_kernel,
        out_shape=(
            jax.ShapeDtypeStruct((owners, cap, width), jnp.bfloat16),
            jax.ShapeDtypeStruct((FACE, width), jnp.bfloat16),
            jax.ShapeDtypeStruct((FACE, width), jnp.bfloat16),
        ),
        grid=(1,),
        in_specs=[
            pl.BlockSpec((comps, nodes, LANES), lambda i: (0, 0, 0)),
            pl.BlockSpec((comps, nodes, LANES), lambda i: (0, 0, last)),
            pl.BlockSpec((cap, owners), lambda i: (0, 0)),
        ],
        out_specs=(
            pl.BlockSpec((owners, cap, width), lambda i: (0, 0, 0)),
            pl.BlockSpec((FACE, width), lambda i: (0, 0)),
            pl.BlockSpec((FACE, width), lambda i: (0, 0)),
        ),
        scratch_shapes=[pltpu.VMEM((width, 2 * LANES), jnp.float32)],
        name="table",
    )(multipoles, multipoles, slots)


def spread_out(y, spread, comp):
    for t in range(spread.shape[1]):
        spread[comp, t] = y[:, t * LANES:(t + 1) * LANES]


def gather_in(total, spread, picks, comp, dirs, nodes):
    tiles = spread.shape[1]
    wide = tiles * LANES
    for d in range(dirs):
        pieces = [spread[comp, t, pl.ds(d, nodes, stride=dirs), :] for t in range(tiles)]
        moved = jnp.concatenate(pieces, axis=1).astype(jnp.bfloat16)
        part = jnp.dot(moved, picks[pl.ds(d * wide, wide), :], preferred_element_type=jnp.float32)
        total = part if total is None else total + part
    return total


def load_kernel(a_hbm, a_ref, sem):
    copy = pltpu.make_async_copy(a_hbm, a_ref, sem)
    copy.start()
    copy.wait()


def near_kernel(m_ref, low_ref, high_ref, codes_ref, a_ref, near_hbm, stage, source, picks, spread, total, out_sems):
    comps, nodes, nboxes = m_ref.shape
    dirs, width = a_ref.shape[1:]
    wide = picks.shape[0] // dirs

    def store(comp):
        return pltpu.make_async_copy(total.at[comp], near_hbm.at[comp], out_sems.at[comp])

    blank = jnp.zeros((wide - nboxes - 2 * FACE, width), jnp.bfloat16)
    source[:, nboxes:] = jnp.concatenate([low_ref[...], high_ref[...], blank], axis=0).T
    place = lax.broadcasted_iota(jnp.int32, (wide, nboxes), 0)
    for d in range(dirs):
        code = codes_ref[pl.ds(d, 1), :]
        low = jnp.where(code < FACE, code + nboxes, code - FACE)
        wanted = jnp.where(code < nboxes + FACE, low, code)
        wanted = jnp.where((code < 0) | (code >= nboxes + 2 * FACE), -1, wanted)
        picks[pl.ds(d * wide, wide), :] = (place == wanted).astype(jnp.bfloat16)
    for comp in range(comps):
        stage[pl.ds(comp * nodes, nodes), :] = m_ref[comp]
    source[:, :nboxes] = stage[...].astype(jnp.bfloat16)

    @pl.loop(0, comps)
    def _(comp):
        a = a_ref[pl.ds(comp * nodes, nodes)].reshape(nodes * dirs, width)
        spread_out(jnp.dot(a, source[...], preferred_element_type=jnp.float32), spread, comp)

    for comp in range(comps):
        total[comp] = gather_in(None, spread, picks, comp, dirs, nodes)
        store(comp).start()
    for comp in range(comps):
        store(comp).wait()


def far_kernel(near_hbm, g_ref, codes_ref, a_hbm, out_hbm, source, picks, spread, held, total, sems, near_sems, out_sems):
    comps, nodes, nboxes = near_hbm.shape
    dirs = a_hbm.shape[1]
    width = a_hbm.shape[2]
    wide = picks.shape[0] // dirs

    def fetch(comp):
        return pltpu.make_async_copy(a_hbm.at[pl.ds(comp * nodes, nodes)], held.at[comp], sems.at[comp])

    def fetch_near(comp):
        return pltpu.make_async_copy(near_hbm.at[comp], total.at[comp], near_sems.at[comp])

    def store(comp):
        return pltpu.make_async_copy(total.at[comp], out_hbm.at[comp], out_sems.at[comp])

    for comp in range(comps):
        fetch(comp).start()
    for comp in range(comps):
        fetch_near(comp).start()
    source[...] = g_ref[...].reshape(source.shape[1], source.shape[0]).T
    place = lax.broadcasted_iota(jnp.int32, (wide, nboxes), 0) + (nboxes + 2 * FACE)
    for d in range(dirs):
        picks[pl.ds(d * wide, wide), :] = (place == codes_ref[pl.ds(d, 1), :]).astype(jnp.bfloat16)

    @pl.loop(0, comps)
    def _(comp):
        fetch(comp).wait()
        a = held[comp].reshape(nodes * dirs, width)
        spread_out(jnp.dot(a, source[...], preferred_element_type=jnp.float32), spread, comp)

    for comp in range(comps):
        fetch_near(comp).wait()
        total[comp] = gather_in(total[comp], spread, picks, comp, dirs, nodes)
        store(comp).start()
    for comp in range(comps):
        store(comp).wait()


HBM = pl.BlockSpec(memory_space=pltpu.MemorySpace.HBM)
VMEM = pl.BlockSpec(memory_space=pltpu.MemorySpace.VMEM)


def near_sum(multipoles, low, high, codes, rows):
    comps, nodes, nboxes = multipoles.shape
    width, dirs, _ = rows.shape
    wide = nboxes + LANES
    rows = pl.pallas_call(
        load_kernel,
        out_shape=jax.ShapeDtypeStruct(rows.shape, rows.dtype),
        in_specs=[HBM],
        out_specs=VMEM,
        scratch_shapes=[pltpu.SemaphoreType.DMA],
        compiler_params=pltpu.CompilerParams(vmem_limit_bytes=45_000_000),
        name="load",
    )(rows)
    return pl.pallas_call(
        near_kernel,
        out_shape=pltpu.MemorySpace.HBM((comps, nodes, nboxes), jnp.float32),
        in_specs=[VMEM, VMEM, VMEM, VMEM, VMEM],
        out_specs=HBM,
        scratch_shapes=[
            pltpu.VMEM((width, nboxes), jnp.float32),
            pltpu.VMEM((width, wide), jnp.bfloat16),
            pltpu.VMEM((dirs * wide, nboxes), jnp.bfloat16),
            pltpu.VMEM((comps, wide // LANES, nodes * dirs, LANES), jnp.float32),
            pltpu.VMEM((comps, nodes, nboxes), jnp.float32),
            pltpu.SemaphoreType.DMA((comps,)),
        ],
        compiler_params=pltpu.CompilerParams(vmem_limit_bytes=30 << 20),
        name="near",
    )(multipoles, low, high, codes, rows)


def far_sum(near, ghost, codes, rows):
    comps, nodes, nboxes = near.shape
    width, dirs, _ = rows.shape
    owners, cap, _ = ghost.shape
    wide = owners * cap
    return pl.pallas_call(
        far_kernel,
        out_shape=jax.ShapeDtypeStruct((comps, nodes, nboxes), jnp.float32),
        in_specs=[HBM, VMEM, VMEM, HBM],
        out_specs=HBM,
        scratch_shapes=[
            pltpu.VMEM((width, wide), jnp.bfloat16),
            pltpu.VMEM((dirs * wide, nboxes), jnp.bfloat16),
            pltpu.VMEM((comps, wide // LANES, nodes * dirs, LANES), jnp.float32),
            pltpu.VMEM((comps, nodes, dirs, width), jnp.bfloat16),
            pltpu.VMEM((comps, nodes, nboxes), jnp.float32),
            pltpu.SemaphoreType.DMA((comps,)),
            pltpu.SemaphoreType.DMA((comps,)),
            pltpu.SemaphoreType.DMA((comps,)),
        ],
        compiler_params=pltpu.CompilerParams(vmem_limit_bytes=52 << 20),
        name="far",
    )(near, ghost, codes, rows)


def local(multipoles, operators, lists, send_slots):
    slots = jnp.transpose(send_slots[0])
    table, low, high = make_table(multipoles, slots)
    ghost = lax.all_to_all(table, "owner", 0, 0, tiled=True)
    count = lax.axis_size("leaf")
    forward = [(i, i + 1) for i in range(count - 1)]
    backward = [(target, source) for source, target in forward]
    low = lax.ppermute(low, "leaf", forward)
    high = lax.ppermute(high, "leaf", backward)
    codes = jnp.transpose(lists)
    rows = jnp.transpose(operators, (1, 0, 2))
    near = near_sum(multipoles, low, high, codes, rows)
    return far_sum(near, ghost, codes, rows)


def solution(mesh):
    return jax.shard_map(
        local,
        mesh=mesh,
        in_specs=(
            P(None, None, ("leaf", "owner")),
            P(),
            P(("leaf", "owner"), None),
            P(("leaf", "owner"), None, None),
        ),
        out_specs=P(None, None, ("leaf", "owner")),
        check_vma=False,
    )
```

```python
import jax
import jax.numpy as jnp
from jax import lax
from jax.experimental import pallas as pl
from jax.experimental.pallas import tpu as pltpu
from jax.sharding import PartitionSpec as P

FACE = 16
LANES = 128
NT = (((1,), (1,)), ((), ()))


def table_kernel(first_ref, last_ref, slots_ref, table_ref, low_ref, high_ref, stage):
    comps, nodes, lanes = first_ref.shape
    cap, owners = slots_ref.shape
    rows = owners * cap
    for comp in range(comps):
        stage[pl.ds(comp * nodes, nodes), :lanes] = first_ref[comp]
        stage[pl.ds(comp * nodes, nodes), lanes:] = last_ref[comp]
    boundary = stage[...].astype(jnp.bfloat16)
    row = lax.broadcasted_iota(jnp.int32, (rows, owners), 0)
    owner = lax.broadcasted_iota(jnp.int32, (rows, owners), 1)
    spread = (row // cap == owner).astype(jnp.bfloat16)
    slots = slots_ref[...].astype(jnp.float32).astype(jnp.bfloat16)
    every = lax.dot_general(spread, slots, NT, preferred_element_type=jnp.float32)
    place = lax.broadcasted_iota(jnp.int32, (rows, cap), 1)
    turn = lax.broadcasted_iota(jnp.int32, (rows, cap), 0) % cap
    wanted = jnp.sum(jnp.where(place == turn, every, 0.0), axis=1, keepdims=True)
    slot = lax.broadcasted_iota(jnp.int32, (rows, 2 * lanes), 1).astype(jnp.float32)
    pick = (slot == wanted).astype(jnp.bfloat16)
    column = lax.broadcasted_iota(jnp.int32, (2 * FACE, 2 * lanes), 1)
    face = lax.broadcasted_iota(jnp.int32, (2 * FACE, 2 * lanes), 0)
    face = jnp.where(face < FACE, face + (2 * lanes - FACE), face - FACE)
    pick = jnp.concatenate([pick, (column == face).astype(jnp.bfloat16)], axis=0)
    table = lax.dot_general(pick, boundary, NT, preferred_element_type=jnp.float32).astype(jnp.bfloat16)
    table_ref[...] = table[:rows].reshape(table_ref.shape)
    low_ref[...] = table[rows:rows + FACE]
    high_ref[...] = table[rows + FACE:]


def make_table(multipoles, slots):
    comps, nodes, nboxes = multipoles.shape
    cap, owners = slots.shape
    width = comps * nodes
    last = nboxes // LANES - 1
    return pl.pallas_call(
        table_kernel,
        out_shape=(
            jax.ShapeDtypeStruct((owners, cap, width), jnp.bfloat16),
            jax.ShapeDtypeStruct((FACE, width), jnp.bfloat16),
            jax.ShapeDtypeStruct((FACE, width), jnp.bfloat16),
        ),
        grid=(1,),
        in_specs=[
            pl.BlockSpec((comps, nodes, LANES), lambda i: (0, 0, 0)),
            pl.BlockSpec((comps, nodes, LANES), lambda i: (0, 0, last)),
            pl.BlockSpec((cap, owners), lambda i: (0, 0)),
        ],
        out_specs=(
            pl.BlockSpec((owners, cap, width), lambda i: (0, 0, 0)),
            pl.BlockSpec((FACE, width), lambda i: (0, 0)),
            pl.BlockSpec((FACE, width), lambda i: (0, 0)),
        ),
        scratch_shapes=[pltpu.VMEM((width, 2 * LANES), jnp.float32)],
        name="table",
    )(multipoles, multipoles, slots)


def spread_out(y, spread, comp):
    for t in range(spread.shape[1]):
        spread[comp, t] = y[:, t * LANES:(t + 1) * LANES]


def gather_in(total, spread, picks, comp, dirs, nodes):
    tiles = spread.shape[1]
    wide = tiles * LANES
    for d in range(dirs):
        pieces = [spread[comp, t, pl.ds(d, nodes, stride=dirs), :] for t in range(tiles)]
        moved = jnp.concatenate(pieces, axis=1).astype(jnp.bfloat16)
        part = jnp.dot(moved, picks[pl.ds(d * wide, wide), :], preferred_element_type=jnp.float32)
        total = part if total is None else total + part
    return total


def stack(stage, block):
    comps, nodes, _ = block.shape
    for comp in range(comps):
        stage[pl.ds(comp * nodes, nodes), :] = block[comp]
    return stage[...].astype(jnp.bfloat16)


def own_kernel(m_hbm, codes_ref, a_hbm, part_hbm, a_ref, block, stage, source, picks, spread, total, m_sem, sems, out_sems):
    comps, nodes, nboxes = total.shape
    dirs, width = a_hbm.shape[1:]
    wide = source.shape[1]

    def fetch(comp):
        rows = pl.ds(comp * nodes, nodes)
        return pltpu.make_async_copy(a_hbm.at[rows], a_ref.at[rows], sems.at[comp])

    def store(comp):
        return pltpu.make_async_copy(total.at[comp], part_hbm.at[comp], out_sems.at[comp])

    load = pltpu.make_async_copy(m_hbm.at[:, :, :wide], block, m_sem)
    load.start()
    for comp in range(comps):
        fetch(comp).start()
    place = lax.broadcasted_iota(jnp.int32, (wide, nboxes), 0) + FACE
    for d in range(dirs):
        picks[pl.ds(d * wide, wide), :] = (place == codes_ref[pl.ds(d, 1), :]).astype(jnp.bfloat16)
    load.wait()
    source[...] = stack(stage, block)

    @pl.loop(0, comps)
    def _(comp):
        fetch(comp).wait()
        a = a_ref[pl.ds(comp * nodes, nodes)].reshape(nodes * dirs, width)
        spread_out(jnp.dot(a, source[...], preferred_element_type=jnp.float32), spread, comp)

    for comp in range(comps):
        total[comp] = gather_in(None, spread, picks, comp, dirs, nodes)
        store(comp).start()
    for comp in range(comps):
        store(comp).wait()


def rim_kernel(part_hbm, m_hbm, low_ref, high_ref, codes_ref, a_ref, near_hbm, block, stage, source, picks, spread, total, m_sem, sems, out_sems):
    comps, nodes, nboxes = total.shape
    dirs, width = a_ref.shape[1:]
    wide = source.shape[1]
    tail = block.shape[2]
    first = nboxes - tail

    def fetch(comp):
        return pltpu.make_async_copy(part_hbm.at[comp], total.at[comp], sems.at[comp])

    def store(comp):
        return pltpu.make_async_copy(total.at[comp], near_hbm.at[comp], out_sems.at[comp])

    load = pltpu.make_async_copy(m_hbm.at[:, :, first:], block, m_sem)
    load.start()
    for comp in range(comps):
        fetch(comp).start()
    blank = jnp.zeros((wide - tail - 2 * FACE, width), jnp.bfloat16)
    source[:, tail:] = jnp.concatenate([low_ref[...], high_ref[...], blank], axis=0).T
    place = lax.broadcasted_iota(jnp.int32, (wide, nboxes), 0)
    for d in range(dirs):
        code = codes_ref[pl.ds(d, 1), :]
        inner = jnp.where(code < nboxes + FACE, code - (first + FACE), code - first)
        wanted = jnp.where(code < FACE, code + tail, inner)
        wanted = jnp.where((code < 0) | (code >= nboxes + 2 * FACE), -1, wanted)
        picks[pl.ds(d * wide, wide), :] = (place == wanted).astype(jnp.bfloat16)
    load.wait()
    source[:, :tail] = stack(stage, block)

    @pl.loop(0, comps)
    def _(comp):
        a = a_ref[pl.ds(comp * nodes, nodes)].reshape(nodes * dirs, width)
        spread_out(jnp.dot(a, source[...], preferred_element_type=jnp.float32), spread, comp)

    for comp in range(comps):
        fetch(comp).wait()
        total[comp] = gather_in(total[comp], spread, picks, comp, dirs, nodes)
        store(comp).start()
    for comp in range(comps):
        store(comp).wait()


def far_kernel(near_hbm, g_ref, codes_ref, a_hbm, out_hbm, source, picks, spread, held, total, sems, near_sems, out_sems):
    comps, nodes, nboxes = near_hbm.shape
    dirs = a_hbm.shape[1]
    width = a_hbm.shape[2]
    wide = picks.shape[0] // dirs

    def fetch(comp):
        return pltpu.make_async_copy(a_hbm.at[pl.ds(comp * nodes, nodes)], held.at[comp], sems.at[comp])

    def fetch_near(comp):
        return pltpu.make_async_copy(near_hbm.at[comp], total.at[comp], near_sems.at[comp])

    def store(comp):
        return pltpu.make_async_copy(total.at[comp], out_hbm.at[comp], out_sems.at[comp])

    for comp in range(comps):
        fetch(comp).start()
    for comp in range(comps):
        fetch_near(comp).start()
    source[...] = g_ref[...].reshape(source.shape[1], source.shape[0]).T
    place = lax.broadcasted_iota(jnp.int32, (wide, nboxes), 0) + (nboxes + 2 * FACE)
    for d in range(dirs):
        picks[pl.ds(d * wide, wide), :] = (place == codes_ref[pl.ds(d, 1), :]).astype(jnp.bfloat16)

    @pl.loop(0, comps)
    def _(comp):
        fetch(comp).wait()
        a = held[comp].reshape(nodes * dirs, width)
        spread_out(jnp.dot(a, source[...], preferred_element_type=jnp.float32), spread, comp)

    for comp in range(comps):
        fetch_near(comp).wait()
        total[comp] = gather_in(total[comp], spread, picks, comp, dirs, nodes)
        store(comp).start()
    for comp in range(comps):
        store(comp).wait()


HBM = pl.BlockSpec(memory_space=pltpu.MemorySpace.HBM)
VMEM = pl.BlockSpec(memory_space=pltpu.MemorySpace.VMEM)


def near_sum(multipoles, low, high, codes, rows):
    shape = multipoles.shape
    comps, nodes, nboxes = shape
    width, dirs, _ = rows.shape
    wide = 2 * LANES
    tail = nboxes - wide

    def scratch(lanes):
        return [
            pltpu.VMEM((comps, nodes, lanes), jnp.float32),
            pltpu.VMEM((width, lanes), jnp.float32),
            pltpu.VMEM((width, wide), jnp.bfloat16),
            pltpu.VMEM((dirs * wide, nboxes), jnp.bfloat16),
            pltpu.VMEM((comps, wide // LANES, nodes * dirs, LANES), jnp.float32),
            pltpu.VMEM(shape, jnp.float32),
            pltpu.SemaphoreType.DMA,
            pltpu.SemaphoreType.DMA((comps,)),
            pltpu.SemaphoreType.DMA((comps,)),
        ]

    part, rows = pl.pallas_call(
        own_kernel,
        out_shape=(
            jax.ShapeDtypeStruct(shape, jnp.float32),
            jax.ShapeDtypeStruct(rows.shape, rows.dtype),
        ),
        in_specs=[HBM, VMEM, HBM],
        out_specs=(HBM, VMEM),
        scratch_shapes=scratch(wide),
        compiler_params=pltpu.CompilerParams(vmem_limit_bytes=42_000_000),
        name="own",
    )(multipoles, codes, rows)
    return pl.pallas_call(
        rim_kernel,
        out_shape=pltpu.MemorySpace.HBM(shape, jnp.float32),
        in_specs=[HBM, HBM, VMEM, VMEM, VMEM, VMEM],
        out_specs=HBM,
        scratch_shapes=scratch(tail),
        compiler_params=pltpu.CompilerParams(vmem_limit_bytes=30 << 20),
        name="rim",
    )(part, multipoles, low, high, codes, rows)


def far_sum(near, ghost, codes, rows):
    comps, nodes, nboxes = near.shape
    width, dirs, _ = rows.shape
    owners, cap, _ = ghost.shape
    wide = owners * cap
    return pl.pallas_call(
        far_kernel,
        out_shape=jax.ShapeDtypeStruct((comps, nodes, nboxes), jnp.float32),
        in_specs=[HBM, VMEM, VMEM, HBM],
        out_specs=HBM,
        scratch_shapes=[
            pltpu.VMEM((width, wide), jnp.bfloat16),
            pltpu.VMEM((dirs * wide, nboxes), jnp.bfloat16),
            pltpu.VMEM((comps, wide // LANES, nodes * dirs, LANES), jnp.float32),
            pltpu.VMEM((comps, nodes, dirs, width), jnp.bfloat16),
            pltpu.VMEM((comps, nodes, nboxes), jnp.float32),
            pltpu.SemaphoreType.DMA((comps,)),
            pltpu.SemaphoreType.DMA((comps,)),
            pltpu.SemaphoreType.DMA((comps,)),
        ],
        compiler_params=pltpu.CompilerParams(vmem_limit_bytes=52 << 20),
        name="far",
    )(near, ghost, codes, rows)


def local(multipoles, operators, lists, send_slots):
    slots = jnp.transpose(send_slots[0])
    table, low, high = make_table(multipoles, slots)
    ghost = lax.all_to_all(table, "owner", 0, 0, tiled=True)
    count = lax.axis_size("leaf")
    forward = [(i, i + 1) for i in range(count - 1)]
    backward = [(target, source) for source, target in forward]
    low = lax.ppermute(low, "leaf", forward)
    high = lax.ppermute(high, "leaf", backward)
    codes = jnp.transpose(lists)
    rows = jnp.transpose(operators, (1, 0, 2))
    near = near_sum(multipoles, low, high, codes, rows)
    return far_sum(near, ghost, codes, rows)


def solution(mesh):
    return jax.shard_map(
        local,
        mesh=mesh,
        in_specs=(
            P(None, None, ("leaf", "owner")),
            P(),
            P(("leaf", "owner"), None),
            P(("leaf", "owner"), None, None),
        ),
        out_specs=P(None, None, ("leaf", "owner")),
        check_vma=False,
    )
```

```python
import jax
import jax.numpy as jnp
from jax import lax
from jax.experimental import pallas as pl
from jax.experimental.pallas import tpu as pltpu
from jax.sharding import PartitionSpec as P

FACE = 16
LANES = 128
NT = (((1,), (1,)), ((), ()))


def table_kernel(first_ref, last_ref, slots_ref, table_ref, low_ref, high_ref, stage):
    comps, nodes, lanes = first_ref.shape
    cap, owners = slots_ref.shape
    rows = owners * cap
    for comp in range(comps):
        stage[pl.ds(comp * nodes, nodes), :lanes] = first_ref[comp]
        stage[pl.ds(comp * nodes, nodes), lanes:] = last_ref[comp]
    boundary = stage[...].astype(jnp.bfloat16)
    row = lax.broadcasted_iota(jnp.int32, (rows, owners), 0)
    owner = lax.broadcasted_iota(jnp.int32, (rows, owners), 1)
    spread = (row // cap == owner).astype(jnp.bfloat16)
    slots = slots_ref[...].astype(jnp.float32).astype(jnp.bfloat16)
    every = lax.dot_general(spread, slots, NT, preferred_element_type=jnp.float32)
    place = lax.broadcasted_iota(jnp.int32, (rows, cap), 1)
    turn = lax.broadcasted_iota(jnp.int32, (rows, cap), 0) % cap
    wanted = jnp.sum(jnp.where(place == turn, every, 0.0), axis=1, keepdims=True)
    slot = lax.broadcasted_iota(jnp.int32, (rows, 2 * lanes), 1).astype(jnp.float32)
    pick = (slot == wanted).astype(jnp.bfloat16)
    column = lax.broadcasted_iota(jnp.int32, (2 * FACE, 2 * lanes), 1)
    face = lax.broadcasted_iota(jnp.int32, (2 * FACE, 2 * lanes), 0)
    face = jnp.where(face < FACE, face + (2 * lanes - FACE), face - FACE)
    pick = jnp.concatenate([pick, (column == face).astype(jnp.bfloat16)], axis=0)
    table = lax.dot_general(pick, boundary, NT, preferred_element_type=jnp.float32).astype(jnp.bfloat16)
    table_ref[...] = table[:rows].reshape(table_ref.shape)
    low_ref[...] = table[rows:rows + FACE]
    high_ref[...] = table[rows + FACE:]


def make_table(multipoles, slots):
    comps, nodes, nboxes = multipoles.shape
    cap, owners = slots.shape
    width = comps * nodes
    last = nboxes // LANES - 1
    return pl.pallas_call(
        table_kernel,
        out_shape=(
            jax.ShapeDtypeStruct((owners, cap, width), jnp.bfloat16),
            jax.ShapeDtypeStruct((FACE, width), jnp.bfloat16),
            jax.ShapeDtypeStruct((FACE, width), jnp.bfloat16),
        ),
        grid=(1,),
        in_specs=[
            pl.BlockSpec((comps, nodes, LANES), lambda i: (0, 0, 0)),
            pl.BlockSpec((comps, nodes, LANES), lambda i: (0, 0, last)),
            pl.BlockSpec((cap, owners), lambda i: (0, 0)),
        ],
        out_specs=(
            pl.BlockSpec((owners, cap, width), lambda i: (0, 0, 0)),
            pl.BlockSpec((FACE, width), lambda i: (0, 0)),
            pl.BlockSpec((FACE, width), lambda i: (0, 0)),
        ),
        scratch_shapes=[pltpu.VMEM((width, 2 * LANES), jnp.float32)],
        name="table",
    )(multipoles, multipoles, slots)


def spread_out(y, spread, comp):
    for t in range(spread.shape[1]):
        spread[comp, t] = y[:, t * LANES:(t + 1) * LANES]


def gather_in(total, spread, picks, comp, dirs, nodes):
    tiles = spread.shape[1]
    wide = tiles * LANES
    for d in range(dirs):
        pieces = [spread[comp, t, pl.ds(d, nodes, stride=dirs), :] for t in range(tiles)]
        moved = jnp.concatenate(pieces, axis=1).astype(jnp.bfloat16)
        part = jnp.dot(moved, picks[pl.ds(d * wide, wide), :], preferred_element_type=jnp.float32)
        total = part if total is None else total + part
    return total


def stack(stage, block):
    comps, nodes, _ = block.shape
    for comp in range(comps):
        stage[pl.ds(comp * nodes, nodes), :] = block[comp]
    return stage[...].astype(jnp.bfloat16)


def own_kernel(m_hbm, codes_ref, a_hbm, part_hbm, a_ref, block, stage, source, picks, spread, total, m_sem, sems, out_sems):
    comps, nodes, nboxes = total.shape
    dirs, width = a_hbm.shape[1:]
    wide = source.shape[1]

    def fetch(comp):
        rows = pl.ds(comp * nodes, nodes)
        return pltpu.make_async_copy(a_hbm.at[rows], a_ref.at[rows], sems.at[comp])

    def store(comp):
        return pltpu.make_async_copy(total.at[comp], part_hbm.at[comp], out_sems.at[comp])

    load = pltpu.make_async_copy(m_hbm.at[:, :, :wide], block, m_sem)
    load.start()
    for comp in range(comps):
        fetch(comp).start()
    place = lax.broadcasted_iota(jnp.int32, (wide, nboxes), 0) + FACE
    for d in range(dirs):
        picks[pl.ds(d * wide, wide), :] = (place == codes_ref[pl.ds(d, 1), :]).astype(jnp.bfloat16)
    load.wait()
    source[...] = stack(stage, block)

    @pl.loop(0, comps)
    def _(comp):
        fetch(comp).wait()
        a = a_ref[pl.ds(comp * nodes, nodes)].reshape(nodes * dirs, width)
        spread_out(jnp.dot(a, source[...], preferred_element_type=jnp.float32), spread, comp)

    for comp in range(comps):
        total[comp] = gather_in(None, spread, picks, comp, dirs, nodes)
        store(comp).start()
    for comp in range(comps):
        store(comp).wait()


def rim_kernel(part_hbm, m_hbm, low_ref, high_ref, codes_ref, a_ref, near_hbm, block, stage, source, picks, spread, total, m_sem, sems, out_sems):
    comps, nodes, nboxes = total.shape
    dirs, width = a_ref.shape[1:]
    wide = source.shape[1]
    tail = block.shape[2]
    first = nboxes - tail

    def fetch(comp):
        return pltpu.make_async_copy(part_hbm.at[comp], total.at[comp], sems.at[comp])

    def store(comp):
        return pltpu.make_async_copy(total.at[comp], near_hbm.at[comp], out_sems.at[comp])

    load = pltpu.make_async_copy(m_hbm.at[:, :, first:], block, m_sem)
    load.start()
    for comp in range(comps):
        fetch(comp).start()
    blank = jnp.zeros((wide - tail - 2 * FACE, width), jnp.bfloat16)
    source[:, tail:] = jnp.concatenate([low_ref[...], high_ref[...], blank], axis=0).T
    place = lax.broadcasted_iota(jnp.int32, (wide, nboxes), 0)
    for d in range(dirs):
        code = codes_ref[pl.ds(d, 1), :]
        inner = jnp.where(code < nboxes + FACE, code - (first + FACE), code - first)
        wanted = jnp.where(code < FACE, code + tail, inner)
        wanted = jnp.where((code < 0) | (code >= nboxes + 2 * FACE), -1, wanted)
        picks[pl.ds(d * wide, wide), :] = (place == wanted).astype(jnp.bfloat16)
    load.wait()
    source[:, :tail] = stack(stage, block)

    @pl.loop(0, comps)
    def _(comp):
        a = a_ref[pl.ds(comp * nodes, nodes)].reshape(nodes * dirs, width)
        spread_out(jnp.dot(a, source[...], preferred_element_type=jnp.float32), spread, comp)

    for comp in range(comps):
        fetch(comp).wait()
        total[comp] = gather_in(total[comp], spread, picks, comp, dirs, nodes)
        store(comp).start()
    for comp in range(comps):
        store(comp).wait()


def far_kernel(near_hbm, g_ref, codes_ref, a_hbm, out_hbm, source, picks, spread, held, total, sems, near_sems, out_sems):
    comps, nodes, nboxes = near_hbm.shape
    dirs = a_hbm.shape[1]
    width = a_hbm.shape[2]
    wide = picks.shape[0] // dirs

    def fetch(comp):
        return pltpu.make_async_copy(a_hbm.at[pl.ds(comp * nodes, nodes)], held.at[comp], sems.at[comp])

    def fetch_near(comp):
        return pltpu.make_async_copy(near_hbm.at[comp], total.at[comp], near_sems.at[comp])

    def store(comp):
        return pltpu.make_async_copy(total.at[comp], out_hbm.at[comp], out_sems.at[comp])

    for comp in range(comps):
        fetch(comp).start(priority=int(comp > 0))
    for comp in range(comps):
        fetch_near(comp).start(priority=1)
    source[...] = g_ref[...].reshape(source.shape[1], source.shape[0]).T
    place = lax.broadcasted_iota(jnp.int32, (wide, nboxes), 0) + (nboxes + 2 * FACE)
    for d in range(dirs):
        picks[pl.ds(d * wide, wide), :] = (place == codes_ref[pl.ds(d, 1), :]).astype(jnp.bfloat16)

    @pl.loop(0, comps)
    def _(comp):
        fetch(comp).wait()
        a = held[comp].reshape(nodes * dirs, width)
        spread_out(jnp.dot(a, source[...], preferred_element_type=jnp.float32), spread, comp)

    for comp in range(comps):
        fetch_near(comp).wait()
        total[comp] = gather_in(total[comp], spread, picks, comp, dirs, nodes)
        store(comp).start()
    for comp in range(comps):
        store(comp).wait()


HBM = pl.BlockSpec(memory_space=pltpu.MemorySpace.HBM)
VMEM = pl.BlockSpec(memory_space=pltpu.MemorySpace.VMEM)


def near_sum(multipoles, low, high, codes, rows):
    shape = multipoles.shape
    comps, nodes, nboxes = shape
    width, dirs, _ = rows.shape
    wide = 2 * LANES
    tail = nboxes - wide

    def scratch(lanes):
        return [
            pltpu.VMEM((comps, nodes, lanes), jnp.float32),
            pltpu.VMEM((width, lanes), jnp.float32),
            pltpu.VMEM((width, wide), jnp.bfloat16),
            pltpu.VMEM((dirs * wide, nboxes), jnp.bfloat16),
            pltpu.VMEM((comps, wide // LANES, nodes * dirs, LANES), jnp.float32),
            pltpu.VMEM(shape, jnp.float32),
            pltpu.SemaphoreType.DMA,
            pltpu.SemaphoreType.DMA((comps,)),
            pltpu.SemaphoreType.DMA((comps,)),
        ]

    part, rows = pl.pallas_call(
        own_kernel,
        out_shape=(
            jax.ShapeDtypeStruct(shape, jnp.float32),
            jax.ShapeDtypeStruct(rows.shape, rows.dtype),
        ),
        in_specs=[HBM, VMEM, HBM],
        out_specs=(HBM, VMEM),
        scratch_shapes=scratch(wide),
        compiler_params=pltpu.CompilerParams(vmem_limit_bytes=42_000_000),
        name="own",
    )(multipoles, codes, rows)
    return pl.pallas_call(
        rim_kernel,
        out_shape=pltpu.MemorySpace.HBM(shape, jnp.float32),
        in_specs=[HBM, HBM, VMEM, VMEM, VMEM, VMEM],
        out_specs=HBM,
        scratch_shapes=scratch(tail),
        compiler_params=pltpu.CompilerParams(vmem_limit_bytes=30 << 20),
        name="rim",
    )(part, multipoles, low, high, codes, rows)


def far_sum(near, ghost, codes, rows):
    comps, nodes, nboxes = near.shape
    width, dirs, _ = rows.shape
    owners, cap, _ = ghost.shape
    wide = owners * cap
    return pl.pallas_call(
        far_kernel,
        out_shape=jax.ShapeDtypeStruct((comps, nodes, nboxes), jnp.float32),
        in_specs=[HBM, VMEM, VMEM, HBM],
        out_specs=HBM,
        scratch_shapes=[
            pltpu.VMEM((width, wide), jnp.bfloat16),
            pltpu.VMEM((dirs * wide, nboxes), jnp.bfloat16),
            pltpu.VMEM((comps, wide // LANES, nodes * dirs, LANES), jnp.float32),
            pltpu.VMEM((comps, nodes, dirs, width), jnp.bfloat16),
            pltpu.VMEM((comps, nodes, nboxes), jnp.float32),
            pltpu.SemaphoreType.DMA((comps,)),
            pltpu.SemaphoreType.DMA((comps,)),
            pltpu.SemaphoreType.DMA((comps,)),
        ],
        compiler_params=pltpu.CompilerParams(vmem_limit_bytes=52 << 20),
        name="far",
    )(near, ghost, codes, rows)


def local(multipoles, operators, lists, send_slots):
    slots = jnp.transpose(send_slots[0])
    table, low, high = make_table(multipoles, slots)
    ghost = lax.all_to_all(table, "owner", 0, 0, tiled=True)
    count = lax.axis_size("leaf")
    forward = [(i, i + 1) for i in range(count - 1)]
    backward = [(target, source) for source, target in forward]
    low = lax.ppermute(low, "leaf", forward)
    high = lax.ppermute(high, "leaf", backward)
    codes = jnp.transpose(lists)
    rows = jnp.transpose(operators, (1, 0, 2))
    near = near_sum(multipoles, low, high, codes, rows)
    return far_sum(near, ghost, codes, rows)


def solution(mesh):
    return jax.shard_map(
        local,
        mesh=mesh,
        in_specs=(
            P(None, None, ("leaf", "owner")),
            P(),
            P(("leaf", "owner"), None),
            P(("leaf", "owner"), None, None),
        ),
        out_specs=P(None, None, ("leaf", "owner")),
        check_vma=False,
    )
```
